256 devices in a mesh: ctx: 32 (over y, z), ch: 8 (over x, core).
Axes of the slice: x: 4, y: 4, z: 8, core: 2. Of those that a mesh axis runs over, the one named last changes fastest.
Arguments:
- queries: float32 [8, 1, 524288], P('ch', None, 'ctx'), may hold values from -6 to 6
- keys: float32 [8, 1, 524288], P('ch', None, 'ctx'), may hold values from -6 to 6
- values: float32 [8, 1, 524288], P('ch', None, 'ctx'), may hold values from -6 to 6
- filters: float32 [1, 524288], P(None, 'ctx'), may hold values from -4 to 4
- cotangent: float32 [8, 1, 524288], P('ch', None, 'ctx'), may hold values from -6 to 6
Outputs:
- mixer_out: float32 [8, 1, 524288], P('ch', None, 'ctx')
- query_grad: float32 [8, 1, 524288], P('ch', None, 'ctx')
- key_grad: float32 [8, 1, 524288], P('ch', None, 'ctx')
- value_grad: float32 [8, 1, 524288], P('ch', None, 'ctx')
- filter_grad: float32 [1, 524288], P(None, ('ctx', 'ch'))
The draws below stay inside these ranges and needn't reach their ends.
All inputs are finite; a program needn't handle non-finite values.
Results may differ from the reference program's by a relative error of at most 0.00013.
Values sent between devices are 32-bit elements; how exact they have to be, the bound alone decides.
A program may use at most 64 MiB of HBM per device.

```python
import math
import jax
import jax.numpy as jnp
from jax import lax

FILTER_COUNT = 1
MEMBERS = 8
SEQUENCE_LENGTH = 524288


def draw_filters(key, part):
    key_rate, key_coin, key_noise, random_key_location, random_key_dropout, key_fast = jax.random.split(key, 6)
    token_offsets = jnp.arange(SEQUENCE_LENGTH, dtype=jnp.float32)[None, :]
    coin_flip = jax.random.uniform(key_coin, (FILTER_COUNT, 1))
    slow_rate = jax.random.uniform(key_rate, (FILTER_COUNT, 1), minval=math.log(0.25 / SEQUENCE_LENGTH), maxval=math.log(2.0 / SEQUENCE_LENGTH))
    fast_rate = jax.random.uniform(key_fast, (FILTER_COUNT, 1), minval=math.log(1.0 / 200.0), maxval=math.log(1.0 / 30.0))
    log_rate = jnp.where(coin_flip < 0.5, fast_rate, slow_rate)
    noise_values = jnp.clip(jax.random.normal(key_noise, (FILTER_COUNT, SEQUENCE_LENGTH)), -4.0, 4.0)
    falloff_speed = jnp.exp(log_rate)
    energy = -jnp.expm1(-2.0 * falloff_speed * SEQUENCE_LENGTH) / -jnp.expm1(-2.0 * falloff_speed)
    spike_positions = jax.random.randint(random_key_location, (FILTER_COUNT, 3, 1), 0, SEQUENCE_LENGTH)
    token_position_index = jnp.arange(SEQUENCE_LENGTH, dtype=jnp.int32)[None, None, :]
    spike_count = jnp.sum((token_position_index >= spike_positions).astype(jnp.float32), axis=1)
    spike_keep_mask = jax.random.uniform(random_key_dropout, (FILTER_COUNT, 1), minval=0.5, maxval=0.8)
    decay_profile = jnp.exp(-falloff_speed * token_offsets) * jnp.exp(spike_count * jnp.log(spike_keep_mask))
    return noise_values * jax.lax.rsqrt(energy) * decay_profile


def steps_of(rng, extent, cuts, low, largest):
    level = 1.0
    for axis_at, parts in cuts:
        heights = jax.random.uniform(jax.random.fold_in(jax.random.fold_in(rng, 6), axis_at), (parts,), jnp.float32, low / len(cuts), largest / len(cuts))
        level = level * jnp.repeat(jnp.exp(heights), extent[axis_at] // parts).reshape((-1,) + (1,) * (len(extent) - 1 - axis_at))
    return level


def normal_values(key, dims, scale, reach, cuts=(), kind=jnp.bfloat16):
    values = scale * jax.random.normal(key, dims, jnp.float32)
    if cuts:
        values = values * steps_of(key, dims, cuts, -0.22, 0.18)
    return jnp.clip(values, -reach, reach).astype(kind)


def setup_inputs(seed: int = 0) -> dict:
    key_of = jax.random.split(jax.random.key(seed), 6)
    return {
        "queries": normal_values(key_of[0], (MEMBERS, FILTER_COUNT, SEQUENCE_LENGTH), 1.0, 6.0, ((0, 8), (2, 32)), jnp.float32),
        "keys": normal_values(key_of[1], (MEMBERS, FILTER_COUNT, SEQUENCE_LENGTH), 1.0, 6.0, ((0, 8), (2, 32)), jnp.float32),
        "values": normal_values(key_of[2], (MEMBERS, FILTER_COUNT, SEQUENCE_LENGTH), 1.0, 6.0, ((0, 8), (2, 32)), jnp.float32),
        "filters": draw_filters(jax.random.fold_in(key_of[5], 71), 0),
        "cotangent": normal_values(key_of[4], (MEMBERS, FILTER_COUNT, SEQUENCE_LENGTH), 1.0, 6.0, ((0, 8), (2, 32)), jnp.float32),
    }


def reference(queries, keys, values, filters, cotangent):
    padded_length = 2 * SEQUENCE_LENGTH
    filter_spec = jnp.fft.rfft(filters, n=padded_length, axis=-1)

    def member_pass(operands):
        query_rows, key_rows, value_rows, upstream = operands
        mixed_input = key_rows * value_rows
        grad_in = upstream * query_rows
        mixed_spec = jnp.fft.rfft(mixed_input, n=padded_length, axis=-1)
        grad_spec = jnp.fft.rfft(grad_in, n=padded_length, axis=-1)
        convolved = jnp.fft.irfft(filter_spec * mixed_spec, n=padded_length, axis=-1)[:, :SEQUENCE_LENGTH]
        mixed_grad = jnp.fft.irfft(jnp.conj(filter_spec) * grad_spec, n=padded_length, axis=-1)[:, :SEQUENCE_LENGTH]
        filter_term = jnp.fft.irfft(jnp.conj(mixed_spec) * grad_spec, n=padded_length, axis=-1)[:, :SEQUENCE_LENGTH]
        return (query_rows * convolved, upstream * convolved, mixed_grad * value_rows, mixed_grad * key_rows, filter_term)

    mixer_out, query_grad, key_grad, value_grad, filter_terms = lax.map(member_pass, (queries, keys, values, cotangent))
    filter_grad = jnp.sum(filter_terms, axis=0) * (MEMBERS * SEQUENCE_LENGTH) ** -0.5
    return (mixer_out, query_grad, key_grad, value_grad, filter_grad)
```

```python
import functools
import math

import jax
import jax.numpy as jnp
import ml_dtypes
import numpy as np
from jax import lax
from jax.experimental import pallas as pl
from jax.experimental.pallas import tpu as pltpu
from jax.sharding import PartitionSpec as P

LANES = 128
OWN = 4
MESH = pl.DeviceIdType.MESH
BF16 = jnp.bfloat16


def split(table):
    high = table.astype(ml_dtypes.bfloat16)
    low = (table - high.astype(np.float64)).astype(ml_dtypes.bfloat16)
    return high, low


def tables(blocks):
    rows = blocks * OWN
    length = rows * LANES
    row = np.arange(2 * rows)
    freq = (row // 8) * OWN + row % OWN + 0.25
    imag = (row % 8) >= OWN
    angle = 2.0 * np.pi * freq[:, None] * np.arange(rows)[None, :] / rows
    outer = np.where(imag[:, None], -np.sin(angle), np.cos(angle))
    high, low = split(outer)
    outer_fwd = np.concatenate([high, low, high], axis=1)
    high, low = split(outer.T / length)
    outer_inv = np.concatenate([high, low, high], axis=1)
    lane = np.arange(LANES)
    twist = 2.0 * np.pi * freq[:, None] * lane[None, :] / length
    twist_cos = np.cos(twist).astype(np.float32)
    twist_sin = np.where(imag[:, None], -np.sin(twist), np.sin(twist)).astype(np.float32)
    inner = 2.0 * np.pi * ((lane[:, None] * lane[None, :]) % LANES) / LANES
    high, low = split(np.concatenate([np.cos(inner), np.sin(inner)], axis=1))
    inner_table = np.concatenate([high, high, low], axis=0)
    return outer_fwd, outer_inv, twist_cos, twist_sin, inner_table


def halves(value):
    high = value.astype(BF16)
    low = (value - high.astype(jnp.float32)).astype(BF16)
    return high, low


def dot(lhs, rhs):
    return jnp.dot(lhs, rhs, preferred_element_type=jnp.float32)


def left_product(table, value):
    high, low = halves(value)
    return dot(table, jnp.concatenate([high, high, low], axis=0))


def right_product(value, table):
    high, low = halves(value)
    return dot(jnp.concatenate([high, low, high], axis=1), table)


def swap(value):
    if value.ndim == 3:
        return pltpu.roll(value, OWN, 1)
    return pltpu.roll(value.reshape(-1, 8, LANES), OWN, 1).reshape(value.shape)


def kernel(
    steps, blocks, members, scale,
    query_ref, key_ref, value_ref, filter_ref, cotangent_ref,
    fwd_ref, inv_ref, cos_ref, sin_ref, inner_ref,
    mixer_ref, query_grad_ref, key_grad_ref, value_grad_ref, filter_grad_ref,
    spectra, arrived, results, returned, grads, filters, mixed, terms, shares,
    send_sems, recv_sems,
):
    me = lax.axis_index("ctx")
    member = lax.axis_index("ch")

    barrier = pltpu.get_barrier_semaphore()
    for step in steps:
        pl.semaphore_signal(
            barrier, inc=1, device_id={"ctx": lax.rem(me + step, blocks)}, device_id_type=MESH
        )
    for step in range(1, members):
        pl.semaphore_signal(
            barrier, inc=1, device_id={"ch": lax.rem(member + step, members)}, device_id_type=MESH
        )

    half = lax.broadcasted_iota(jnp.int32, (1, 8, LANES), 1) < OWN
    sign = jnp.where(half, 1.0, -1.0).astype(jnp.float32)
    row_sign = jnp.broadcast_to(sign, (2 * blocks // 2, 8, LANES)).reshape(-1, LANES)

    def forward(value):
        rows = left_product(fwd_ref[...], value)
        rows = cos_ref[...] * rows + sin_ref[...] * swap(rows)
        both = right_product(rows, inner_ref[...])
        return both[:, :LANES] + row_sign * swap(both[:, LANES:])

    def inverse(rows):
        both = right_product(rows, inner_ref[...])
        rows = both[:, :LANES] - row_sign * swap(both[:, LANES:])
        rows = cos_ref[...] * rows - sin_ref[...] * swap(rows)
        return left_product(inv_ref[...], rows)

    def exchange(source, target, slot, part):
        copies = []
        for at, step in enumerate(steps):
            peer = lax.rem(me + step, blocks)
            copies.append(
                pltpu.make_async_remote_copy(
                    src_ref=source.at[peer, part],
                    dst_ref=target.at[me, part],
                    send_sem=send_sems.at[slot, at],
                    recv_sem=recv_sems.at[slot, at],
                    device_id={"ctx": peer},
                    device_id_type=MESH,
                )
            )
        return copies

    mixed_input = key_ref[...] * value_ref[...]
    grad_in = cotangent_ref[...] * query_ref[...]
    for at, value in enumerate((mixed_input, grad_in, filter_ref[...])):
        spectra[:, at] = forward(value).reshape(blocks, 8, LANES)

    pl.semaphore_wait(barrier, blocks + members - 2)

    sent = exchange(spectra, arrived, 0, pl.ds(0, 3))
    for copy in sent:
        copy.start()
    arrived[me] = spectra[me]

    group = min(8, blocks)
    zeros = jnp.zeros((group, 8, LANES), jnp.float32)
    for copy in sent:
        copy.wait_recv()

    def shifted(value):
        before = jnp.concatenate([jnp.zeros_like(value[:1]), value[:-1]], axis=0)
        return value - sign * swap(before)

    def factors(value):
        other = swap(value)
        return jnp.where(half, value, other), sign * jnp.where(half, other, value)

    grad = arrived[:, 1]
    grads[0, :blocks] = grad
    grads[1, :blocks] = swap(grad)
    grads[0, blocks:] = zeros
    grads[1, blocks:] = zeros
    mix = arrived[:, 0]
    mixed[0, :group] = zeros
    mixed[1, :group] = zeros
    mixed[0, group:] = mix
    mixed[1, group:] = swap(mix)
    real, imag = factors(shifted(mix))
    terms[0] = real
    terms[1] = imag
    real, imag = factors(shifted(arrived[:, 2]))
    filters[0] = real
    filters[1] = imag

    def correlate(factor, first):
        def add(at, total):
            window = pl.ds(first + at, group)
            return total + grads[0, window] * factor[0, at] + grads[1, window] * factor[1, at]
        return lax.fori_loop(0, blocks - first, add, zeros)

    def convolve(first):
        def add(at, total):
            window = pl.ds(group + first - at, group)
            return total + mixed[0, window] * filters[0, at] - mixed[1, window] * filters[1, at]
        return lax.fori_loop(0, first + group, add, zeros)

    for first in range(0, blocks, group):
        results[pl.ds(first, group), 0] = correlate(terms, first)
    sent_terms = exchange(results, returned, 1, pl.ds(0, 1))
    for copy in sent_terms:
        copy.start()
    for first in range(0, blocks, group):
        results[pl.ds(first, group), 1] = convolve(first)
        results[pl.ds(first, group), 2] = correlate(filters, first)
    sent_results = exchange(results, returned, 2, pl.ds(1, 2))
    for copy in sent_results:
        copy.start()
    returned[me] = results[me]

    for copy in sent_terms:
        copy.wait_recv()
    term = inverse(returned[:, 0].reshape(-1, LANES)) * scale
    shares[0] = term.reshape((members,) + shares.shape[2:])
    sent_shares = []
    for step in range(1, members):
        peer = lax.rem(member + step, members)
        sent_shares.append(
            pltpu.make_async_remote_copy(
                src_ref=shares.at[0, peer],
                dst_ref=shares.at[1, step],
                send_sem=send_sems.at[3, step],
                recv_sem=recv_sems.at[3, step],
                device_id={"ch": peer},
                device_id_type=MESH,
            )
        )
    for copy in sent_shares:
        copy.start()

    for copy in sent_results:
        copy.wait_recv()
    convolved = inverse(returned[:, 1].reshape(-1, LANES))
    mixer_ref[...] = query_ref[...] * convolved
    query_grad_ref[...] = cotangent_ref[...] * convolved
    mixed_grad = inverse(returned[:, 2].reshape(-1, LANES))
    key_grad_ref[...] = mixed_grad * value_ref[...]
    value_grad_ref[...] = mixed_grad * key_ref[...]

    total = shares[0, member]
    for copy in sent_shares:
        copy.wait_recv()
    for step in range(1, members):
        total = total + shares[1, step]
    filter_grad_ref[...] = total
    for copy in sent + sent_terms + sent_results + sent_shares:
        copy.wait_send()


def body(queries, keys, values, filters, cotangent):
    blocks = lax.axis_size("ctx")
    members = lax.axis_size("ch")
    rows = blocks * OWN
    share = rows // members
    group = min(8, blocks)
    tokens = queries.shape[-1]
    scale = (members * queries.shape[0] * blocks * tokens) ** -0.5
    steps = list(range(1, blocks))
    block = jax.ShapeDtypeStruct((rows, LANES), jnp.float32)
    view = lambda array: array.reshape(rows, LANES)
    vmem = pl.BlockSpec(memory_space=pltpu.VMEM)
    outputs = pl.pallas_call(
        functools.partial(kernel, steps, blocks, members, scale),
        out_shape=[block] * 4 + [jax.ShapeDtypeStruct((share, LANES), jnp.float32)],
        in_specs=[vmem] * 10,
        out_specs=[vmem] * 5,
        scratch_shapes=[
            pltpu.VMEM((blocks, 3, 8, LANES), jnp.float32),
            pltpu.VMEM((blocks, 3, 8, LANES), jnp.float32),
            pltpu.VMEM((blocks, 3, 8, LANES), jnp.float32),
            pltpu.VMEM((blocks, 3, 8, LANES), jnp.float32),
            pltpu.VMEM((2, blocks + group, 8, LANES), jnp.float32),
            pltpu.VMEM((2, blocks, 8, LANES), jnp.float32),
            pltpu.VMEM((2, blocks + group, 8, LANES), jnp.float32),
            pltpu.VMEM((2, blocks, 8, LANES), jnp.float32),
            pltpu.VMEM((2, members, share, LANES), jnp.float32),
            pltpu.SemaphoreType.DMA((4, blocks)),
            pltpu.SemaphoreType.DMA((4, blocks)),
        ],
        compiler_params=pltpu.CompilerParams(collective_id=0, has_side_effects=True),
    )(*map(view, (queries, keys, values, filters, cotangent)), *map(jnp.asarray, tables(blocks)))
    mixer_out, query_grad, key_grad, value_grad, filter_grad = outputs
    full = lambda array: array.reshape(queries.shape)
    return (
        full(mixer_out), full(query_grad), full(key_grad), full(value_grad),
        filter_grad.reshape(1, tokens // members),
    )


def solution(mesh):
    placed = (
        P("ch", None, "ctx"),
        P("ch", None, "ctx"),
        P("ch", None, "ctx"),
        P(None, "ctx"),
        P("ch", None, "ctx"),
    )
    return jax.shard_map(
        body,
        mesh=mesh,
        in_specs=placed,
        out_specs=(
            P("ch", None, "ctx"),
            P("ch", None, "ctx"),
            P("ch", None, "ctx"),
            P("ch", None, "ctx"),
            P(None, ("ctx", "ch")),
        ),
        check_vma=False,
    )
```

```python
import functools
import math

import jax
import jax.numpy as jnp
import ml_dtypes
import numpy as np
from jax import lax
from jax.experimental import pallas as pl
from jax.experimental.pallas import tpu as pltpu
from jax.sharding import PartitionSpec as P

LANES = 128
OWN = 4
MESH = pl.DeviceIdType.MESH
BF16 = jnp.bfloat16


def split(table):
    high = table.astype(ml_dtypes.bfloat16)
    low = (table - high.astype(np.float64)).astype(ml_dtypes.bfloat16)
    return high, low


def tables(blocks):
    rows = blocks * OWN
    length = rows * LANES
    row = np.arange(2 * rows)
    freq = (row // 8) * OWN + row % OWN + 0.25
    imag = (row % 8) >= OWN
    angle = 2.0 * np.pi * freq[:, None] * np.arange(rows)[None, :] / rows
    outer = np.where(imag[:, None], -np.sin(angle), np.cos(angle))
    high, low = split(outer)
    outer_fwd = np.concatenate([high, low, high], axis=1)
    high, low = split(outer.T / length)
    outer_inv = np.concatenate([high, low, high], axis=1)
    lane = np.arange(LANES)
    twist = 2.0 * np.pi * freq[:, None] * lane[None, :] / length
    twist_cos = np.cos(twist).astype(np.float32)
    twist_sin = np.where(imag[:, None], -np.sin(twist), np.sin(twist)).astype(np.float32)
    inner = 2.0 * np.pi * ((lane[:, None] * lane[None, :]) % LANES) / LANES
    high, low = split(np.concatenate([np.cos(inner), np.sin(inner)], axis=1))
    inner_table = np.concatenate([high, high, low], axis=0)
    return outer_fwd, outer_inv, twist_cos, twist_sin, inner_table


def halves(value):
    high = value.astype(BF16)
    low = (value - high.astype(jnp.float32)).astype(BF16)
    return high, low


def dot(lhs, rhs):
    return jnp.dot(lhs, rhs, preferred_element_type=jnp.float32)


def left_product(table, value):
    high, low = halves(value)
    return dot(table, jnp.concatenate([high, high, low], axis=0))


def right_product(value, table):
    high, low = halves(value)
    return dot(jnp.concatenate([high, low, high], axis=1), table)


def swap(value):
    if value.ndim == 3:
        return pltpu.roll(value, OWN, 1)
    return pltpu.roll(value.reshape(-1, 8, LANES), OWN, 1).reshape(value.shape)


def kernel(
    blocks, members, scale,
    query_hbm, key_hbm, value_hbm, filter_hbm, cotangent_hbm,
    fwd_hbm, inv_hbm, cos_hbm, sin_hbm, inner_hbm,
    convolved_ref, mixed_grad_ref, filter_grad_ref,
    query_ref, key_ref, value_ref, filter_ref, cotangent_ref,
    fwd_ref, inv_ref, cos_ref, sin_ref, inner_ref,
    spectra, arrived, filter_spectra, filter_arrived,
    results, returned, terms, terms_arrived, term_sums, term_rows, pieces, piece,
    grads, filters, mixed, factor,
    load_sems, pair_send, pair_recv, filter_send, filter_recv, pass_send, pass_recv,
    terms_send, terms_recv, sums_send, sums_recv, result_send, result_recv, piece_send, piece_recv,
):
    me = lax.axis_index("ctx")
    member = lax.axis_index("ch")
    depth = members
    height = blocks // depth
    at_y = lax.div(me, depth)
    at_z = lax.rem(me, depth)

    barrier = pltpu.get_barrier_semaphore()
    for step in range(1, blocks):
        pl.semaphore_signal(
            barrier, inc=1, device_id={"ctx": lax.rem(me + step, blocks)}, device_id_type=MESH
        )
    for step in range(1, members):
        pl.semaphore_signal(
            barrier, inc=1, device_id={"ch": lax.rem(member + step, members)}, device_id_type=MESH
        )

    loads = [
        pltpu.make_async_copy(source, target, load_sems.at[at])
        for at, (source, target) in enumerate((
            (key_hbm, key_ref), (value_hbm, value_ref), (cotangent_hbm, cotangent_ref),
            (query_hbm, query_ref), (fwd_hbm, fwd_ref), (filter_hbm, filter_ref),
            (cos_hbm, cos_ref), (sin_hbm, sin_ref), (inner_hbm, inner_ref), (inv_hbm, inv_ref),
        ))
    ]
    for load in loads:
        load.start()

    half = lax.broadcasted_iota(jnp.int32, (1, 8, LANES), 1) < OWN
    sign = jnp.where(half, 1.0, -1.0).astype(jnp.float32)

    def rows_sign(rows):
        return jnp.broadcast_to(sign, (rows // 8, 8, LANES)).reshape(rows, LANES)

    def forward(values):
        count = len(values)
        rows = left_product(fwd_ref[...], jnp.concatenate(values, axis=1))
        cos, sin = cos_ref[...], sin_ref[...]
        parts = [rows[:, at * LANES : (at + 1) * LANES] for at in range(count)]
        parts = [cos * part + sin * swap(part) for part in parts]
        both = right_product(jnp.concatenate(parts, axis=0), inner_ref[...])
        rows = both[:, :LANES] + rows_sign(count * 8 * blocks) * swap(both[:, LANES:])
        return rows.reshape(count, blocks, 8, LANES)

    def inverse(rows):
        both = right_product(rows, inner_ref[...])
        rows = both[:, :LANES] - rows_sign(8 * blocks) * swap(both[:, LANES:])
        rows = cos_ref[...] * rows - sin_ref[...] * swap(rows)
        return left_product(inv_ref[...], rows)

    def send(source, target, send_sem, recv_sem, **device):
        return pltpu.make_async_remote_copy(
            src_ref=source, dst_ref=target, send_sem=send_sem, recv_sem=recv_sem,
            device_id=device, device_id_type=MESH,
        )

    for load in loads[:9]:
        load.wait()
    mixed_input = key_ref[...] * value_ref[...]
    grad_in = cotangent_ref[...] * query_ref[...]
    filter_spectra[...] = forward([filter_ref[...]])[0]
    pair = forward([mixed_input, grad_in])
    spectra[:, 0] = pair[0]
    spectra[:, 1] = pair[1]

    pl.semaphore_wait(barrier, blocks + members - 2)

    target_z = lax.rem(at_z + member, depth)
    direct = []
    for step in range(height):
        peer = lax.rem(at_y + step, height) * depth + target_z
        direct.append(
            send(
                filter_spectra.at[peer], filter_arrived.at[at_z, at_y],
                filter_send.at[step], filter_recv.at[step], ctx=peer,
            )
        )
    for copy in direct[1:]:
        copy.start()

    @pl.when(member == 0)
    def _():
        filter_arrived[at_z, at_y] = filter_spectra[me]

    @pl.when(member != 0)
    def _():
        direct[0].start()

    pairs = []
    for step in range(1, blocks):
        peer = lax.rem(me + step, blocks)
        pairs.append(
            send(
                spectra.at[peer], arrived.at[me],
                pair_send.at[step], pair_recv.at[step], ctx=peer,
            )
        )
    for copy in pairs:
        copy.start()
    arrived[me] = spectra[me]

    @pl.when(member != 0)
    def _():
        direct[0].wait_recv()

    for copy in direct[1:]:
        copy.wait_recv()
    source_z = lax.rem(at_z - member + depth, depth)
    passed = []
    for step in range(1, members):
        passed.append(
            send(
                filter_arrived.at[source_z], filter_arrived.at[source_z],
                pass_send.at[step], pass_recv.at[step], ch=lax.rem(member + step, members),
            )
        )
    for copy in passed:
        copy.start()

    zeros = jnp.zeros((depth, 8, LANES), jnp.float32)
    grads[0, blocks:] = zeros
    grads[1, blocks:] = zeros
    mixed[0, :depth] = zeros
    mixed[1, :depth] = zeros

    def shifted(value):
        before = jnp.concatenate([jnp.zeros_like(value[:1]), value[:-1]], axis=0)
        return value - sign * swap(before)

    def factors(value):
        other = swap(value)
        return jnp.where(half, value, other), sign * jnp.where(half, other, value)

    unroll = math.gcd(4, depth)

    def correlate(factor, first):
        def add(at, total):
            for more in range(unroll):
                lag = at * unroll + more
                window = pl.ds(first + lag, depth)
                total = total + grads[0, window] * factor[0, lag] + grads[1, window] * factor[1, lag]
            return total
        return lax.fori_loop(0, (blocks - first) // unroll, add, zeros)

    def convolve(first):
        def add(at, total):
            for more in range(unroll):
                lag = at * unroll + more
                window = pl.ds(depth + first - lag, depth)
                total = total + mixed[0, window] * filters[0, lag] - mixed[1, window] * filters[1, lag]
            return total
        return lax.fori_loop(0, (first + depth) // unroll, add, zeros)

    for copy in pairs:
        copy.wait_recv()
    grad = arrived[:, 1]
    grads[0, :blocks] = grad
    grads[1, :blocks] = swap(grad)
    mix = arrived[:, 0]
    mixed[0, depth:] = mix
    mixed[1, depth:] = swap(mix)
    real, imag = factors(shifted(mix))
    factor[0] = real
    factor[1] = imag
    for row in range(height):
        terms[:, row] = correlate(factor, row * depth)
    reduced = []
    for step in range(1, members):
        peer = lax.rem(member + step, members)
        reduced.append(
            send(
                terms.at[peer], terms_arrived.at[step],
                terms_send.at[step], terms_recv.at[step], ch=peer,
            )
        )
    for copy in reduced:
        copy.start()

    for copy in passed:
        copy.wait_recv()
    whole = jnp.concatenate([filter_arrived[:, row] for row in range(height)], axis=0)
    real, imag = factors(shifted(whole))
    filters[0] = real
    filters[1] = imag

    def give_back(part):
        copies = []
        for step in range(1, blocks):
            peer = lax.rem(me + step, blocks)
            copies.append(
                send(
                    results.at[part, peer], returned.at[part, me],
                    result_send.at[part, step], result_recv.at[part, step], ctx=peer,
                )
            )
        for copy in copies:
            copy.start()
        returned[part, me] = results[part, me]
        return copies

    for row in range(height):
        results[0, pl.ds(row * depth, depth)] = convolve(row * depth)
    sent_convolved = give_back(0)

    worker = at_z == member
    for copy in reduced:
        copy.wait_recv()
    total = terms[member]
    for step in range(1, members):
        total = total + terms_arrived[step]
    term_sums[...] = total
    summed = []
    for step in range(height):
        row = lax.rem(at_y + step, height)
        summed.append(
            send(
                term_sums.at[row], term_rows.at[me],
                sums_send.at[step], sums_recv.at[me], ctx=row * depth + member,
            )
        )
    for copy in summed[1:]:
        copy.start()

    @pl.when(worker)
    def _():
        term_rows[me] = term_sums[at_y]

    @pl.when(jnp.logical_not(worker))
    def _():
        summed[0].start()

    for row in range(height):
        results[1, pl.ds(row * depth, depth)] = correlate(filters, row * depth)
    sent_grads = give_back(1)

    loads[9].wait()
    for copy in sent_convolved:
        copy.wait_recv()
    convolved_ref[...] = inverse(returned[0].reshape(-1, LANES))

    scattered = []
    for step in range(1, members):
        peer = lax.rem(member + step, members)
        scattered.append(
            send(pieces.at[peer], piece, piece_send.at[step], piece_recv.at[0], ch=peer)
        )

    @pl.when(worker)
    def _():
        for step in range(1, blocks):
            peer = lax.rem(me + step, blocks)
            send(
                term_sums.at[0], term_rows.at[peer], sums_send.at[0], sums_recv.at[peer], ctx=peer
            ).wait_recv()
        term = inverse(term_rows[...].reshape(-1, LANES)) * scale
        pieces[...] = term.reshape(pieces.shape)
        for copy in scattered:
            copy.start()
        piece[...] = pieces[member]

    for copy in sent_grads:
        copy.wait_recv()
    mixed_grad_ref[...] = inverse(returned[1].reshape(-1, LANES))

    @pl.when(jnp.logical_not(worker))
    def _():
        scattered[0].wait_recv()
        summed[0].wait_send()

    filter_grad_ref[...] = piece[...]

    @pl.when(worker)
    def _():
        for copy in scattered:
            copy.wait_send()

    @pl.when(member != 0)
    def _():
        direct[0].wait_send()

    for copy in direct[1:] + pairs + passed + reduced + sent_convolved + summed[1:] + sent_grads:
        copy.wait_send()


def body(queries, keys, values, filters, cotangent):
    blocks = lax.axis_size("ctx")
    members = lax.axis_size("ch")
    height = blocks // members
    rows = blocks * OWN
    share = rows // members
    tokens = queries.shape[-1]
    scale = (members * queries.shape[0] * blocks * tokens) ** -0.5
    view = lambda array: array.reshape(rows, LANES)
    arrays = [*map(view, (queries, keys, values, filters, cotangent)), *map(jnp.asarray, tables(blocks))]
    anywhere = pl.BlockSpec(memory_space=pl.ANY)
    vmem = lambda *shape: pltpu.VMEM(shape + (8, LANES), jnp.float32)
    dma = lambda *shape: pltpu.SemaphoreType.DMA(shape)
    convolved, mixed_grad, filter_grad = pl.pallas_call(
        functools.partial(kernel, blocks, members, scale),
        out_shape=[pltpu.VMEM((rows, LANES), jnp.float32)] * 2
        + [pltpu.VMEM((share, LANES), jnp.float32)],
        in_specs=[anywhere] * 10,
        out_specs=[pl.BlockSpec(memory_space=pltpu.VMEM)] * 3,
        scratch_shapes=[pltpu.VMEM(array.shape, array.dtype) for array in arrays]
        + [
            vmem(blocks, 2), vmem(blocks, 2), vmem(blocks), vmem(members, height),
            vmem(2, blocks), vmem(2, blocks),
            vmem(members, height), vmem(members, height), vmem(height), vmem(blocks),
            pltpu.VMEM((members, share, LANES), jnp.float32),
            pltpu.VMEM((share, LANES), jnp.float32),
            vmem(2, blocks + members), vmem(2, blocks), vmem(2, blocks + members), vmem(2, blocks),
            dma(10), dma(blocks), dma(blocks), dma(height), dma(height), dma(members), dma(members),
            dma(members), dma(members), dma(height), dma(blocks), dma(2, blocks), dma(2, blocks),
            dma(members), dma(1),
        ],
        compiler_params=pltpu.CompilerParams(collective_id=0, has_side_effects=True),
    )(*arrays)
    convolved = convolved.reshape(queries.shape)
    mixed_grad = mixed_grad.reshape(queries.shape)
    return (
        queries * convolved, cotangent * convolved, mixed_grad * values, mixed_grad * keys,
        filter_grad.reshape(1, tokens // members),
    )


def solution(mesh):
    placed = (
        P("ch", None, "ctx"),
        P("ch", None, "ctx"),
        P("ch", None, "ctx"),
        P(None, "ctx"),
        P("ch", None, "ctx"),
    )
    return jax.shard_map(
        body,
        mesh=mesh,
        in_specs=placed,
        out_specs=(
            P("ch", None, "ctx"),
            P("ch", None, "ctx"),
            P("ch", None, "ctx"),
            P("ch", None, "ctx"),
            P(None, ("ctx", "ch")),
        ),
        check_vma=False,
    )
```

```python
import functools
import math

import jax
import jax.numpy as jnp
import ml_dtypes
import numpy as np
from jax import lax
from jax.experimental import pallas as pl
from jax.experimental.pallas import tpu as pltpu
from jax.sharding import PartitionSpec as P

LANES = 128
OWN = 4
MESH = pl.DeviceIdType.MESH
BF16 = jnp.bfloat16


def split(table):
    high = table.astype(ml_dtypes.bfloat16)
    low = (table - high.astype(np.float64)).astype(ml_dtypes.bfloat16)
    return high, low


def tables(blocks):
    rows = blocks * OWN
    length = rows * LANES
    row = np.arange(2 * rows)
    freq = (row // 8) * OWN + row % OWN + 0.25
    imag = (row % 8) >= OWN
    angle = 2.0 * np.pi * freq[:, None] * np.arange(rows)[None, :] / rows
    outer = np.where(imag[:, None], -np.sin(angle), np.cos(angle))
    high, low = split(outer)
    outer_fwd = np.concatenate([high, low, high], axis=1)
    high, low = split(outer.T / length)
    outer_inv = np.concatenate([high, low, high], axis=1)
    lane = np.arange(LANES)
    twist = 2.0 * np.pi * freq[:, None] * lane[None, :] / length
    twist_cos = np.cos(twist).astype(np.float32)
    twist_sin = np.where(imag[:, None], -np.sin(twist), np.sin(twist)).astype(np.float32)
    inner = 2.0 * np.pi * ((lane[:, None] * lane[None, :]) % LANES) / LANES
    high, low = split(np.concatenate([np.cos(inner), np.sin(inner)], axis=1))
    inner_table = np.concatenate([high, high, low], axis=0)
    return outer_fwd, outer_inv, twist_cos, twist_sin, inner_table


def halves(value):
    high = value.astype(BF16)
    low = (value - high.astype(jnp.float32)).astype(BF16)
    return high, low


def dot(lhs, rhs):
    return jnp.dot(lhs, rhs, preferred_element_type=jnp.float32)


def left_product(table, value):
    high, low = halves(value)
    return dot(table, jnp.concatenate([high, high, low], axis=0))


def right_product(value, table):
    high, low = halves(value)
    return dot(jnp.concatenate([high, low, high], axis=1), table)


def swap(value):
    if value.ndim == 3:
        return pltpu.roll(value, OWN, 1)
    return pltpu.roll(value.reshape(-1, 8, LANES), OWN, 1).reshape(value.shape)


def kernel(
    blocks, members, scale,
    query_hbm, key_hbm, value_hbm, filter_hbm, cotangent_hbm,
    fwd_hbm, inv_hbm, cos_hbm, sin_hbm, inner_hbm,
    convolved_ref, mixed_grad_ref, filter_grad_ref,
    query_ref, key_ref, value_ref, filter_ref, cotangent_ref,
    fwd_ref, inv_ref, cos_ref, sin_ref, inner_ref,
    spectra, arrived, filter_spectra, filter_arrived, results, returned, shares,
    grads, filters, mixed, factor,
    load_sems, filter_send, filter_recv, pass_send, pass_recv,
    block_send, block_recv, share_send, share_recv,
):
    me = lax.axis_index("ctx")
    member = lax.axis_index("ch")
    depth = members
    height = blocks // depth
    at_y = lax.div(me, depth)
    at_z = lax.rem(me, depth)

    def hops(step):
        over_y, over_z = step // depth, step % depth
        return min(over_y, height - over_y) + min(over_z, depth - over_z)

    peers = [
        (step, lax.rem(at_y + step // depth, height) * depth + lax.rem(at_z + step % depth, depth))
        for step in sorted(range(1, blocks), key=lambda step: -hops(step))
    ]
    barrier = pltpu.get_barrier_semaphore()
    for _, peer in peers:
        pl.semaphore_signal(barrier, inc=1, device_id={"ctx": peer}, device_id_type=MESH)
    for step in range(1, members):
        pl.semaphore_signal(
            barrier, inc=1, device_id={"ch": lax.rem(member + step, members)}, device_id_type=MESH
        )

    loads = [
        pltpu.make_async_copy(source, target, load_sems.at[at])
        for at, (source, target) in enumerate((
            (cotangent_hbm, cotangent_ref), (query_hbm, query_ref), (filter_hbm, filter_ref),
            (fwd_hbm, fwd_ref), (cos_hbm, cos_ref), (sin_hbm, sin_ref), (inner_hbm, inner_ref),
            (key_hbm, key_ref), (value_hbm, value_ref), (inv_hbm, inv_ref),
        ))
    ]
    for load in loads:
        load.start()

    half = lax.broadcasted_iota(jnp.int32, (1, 8, LANES), 1) < OWN
    sign = jnp.where(half, 1.0, -1.0).astype(jnp.float32)

    def rows_sign(rows):
        return jnp.broadcast_to(sign, (rows // 8, 8, LANES)).reshape(rows, LANES)

    def forward(values):
        count = len(values)
        rows = left_product(fwd_ref[...], jnp.concatenate(values, axis=1))
        cos, sin = cos_ref[...], sin_ref[...]
        parts = [rows[:, at * LANES : (at + 1) * LANES] for at in range(count)]
        parts = [cos * part + sin * swap(part) for part in parts]
        both = right_product(jnp.concatenate(parts, axis=0), inner_ref[...])
        rows = both[:, :LANES] + rows_sign(count * 8 * blocks) * swap(both[:, LANES:])
        return rows.reshape(count, blocks, 8, LANES)

    def inverse(rows):
        both = right_product(rows, inner_ref[...])
        rows = both[:, :LANES] - rows_sign(8 * blocks) * swap(both[:, LANES:])
        rows = cos_ref[...] * rows - sin_ref[...] * swap(rows)
        return left_product(inv_ref[...], rows)

    def send(source, target, send_sem, recv_sem, **device):
        return pltpu.make_async_remote_copy(
            src_ref=source, dst_ref=target, send_sem=send_sem, recv_sem=recv_sem,
            device_id=device, device_id_type=MESH,
        )

    def exchange(outgoing, incoming, part):
        copies = [
            send(
                outgoing.at[peer], incoming.at[me],
                block_send.at[part, step], block_recv.at[part, step], ctx=peer,
            )
            for step, peer in peers
        ]
        for copy in copies:
            copy.start()
        incoming[me] = outgoing[me]
        return copies

    for load in loads[:9]:
        load.wait()
    pair = forward(
        [cotangent_ref[...] * query_ref[...], key_ref[...] * value_ref[...], filter_ref[...]]
    )
    spectra[:, 0] = pair[0]
    spectra[:, 1] = pair[1]
    filter_spectra[...] = pair[2]

    pl.semaphore_wait(barrier, blocks + members - 2)

    target_z = lax.rem(at_z + member, depth)
    direct = []
    for step in range(height):
        peer = lax.rem(at_y + step, height) * depth + target_z
        direct.append(
            send(
                filter_spectra.at[peer], filter_arrived.at[at_z, at_y],
                filter_send.at[step], filter_recv.at[step], ctx=peer,
            )
        )
    for copy in direct[1:]:
        copy.start()

    @pl.when(member == 0)
    def _():
        filter_arrived[at_z, at_y] = filter_spectra[me]

    @pl.when(member != 0)
    def _():
        direct[0].start()

    sent = exchange(spectra, arrived, 0)

    @pl.when(member != 0)
    def _():
        direct[0].wait_recv()

    for copy in direct[1:]:
        copy.wait_recv()
    source_z = lax.rem(at_z - member + depth, depth)
    passed = []
    for step in range(1, members):
        passed.append(
            send(
                filter_arrived.at[source_z], filter_arrived.at[source_z],
                pass_send.at[step], pass_recv.at[step], ch=lax.rem(member + step, members),
            )
        )
    for copy in passed:
        copy.start()

    zeros = jnp.zeros((depth, 8, LANES), jnp.float32)
    grads[0, blocks:] = zeros
    grads[1, blocks:] = zeros
    mixed[0, :depth] = zeros
    mixed[1, :depth] = zeros

    def shifted(value):
        before = jnp.concatenate([jnp.zeros_like(value[:1]), value[:-1]], axis=0)
        return value - sign * swap(before)

    def factors(value):
        other = swap(value)
        return jnp.where(half, value, other), sign * jnp.where(half, other, value)

    unroll = math.gcd(4, depth)

    def correlate(factor, first):
        def add(at, total):
            for more in range(unroll):
                lag = at * unroll + more
                window = pl.ds(first + lag, depth)
                total = total + grads[0, window] * factor[0, lag] + grads[1, window] * factor[1, lag]
            return total
        return lax.fori_loop(0, (blocks - first) // unroll, add, zeros)

    def convolve(first):
        def add(at, total):
            for more in range(unroll):
                lag = at * unroll + more
                window = pl.ds(depth + first - lag, depth)
                total = total + mixed[0, window] * filters[0, lag] - mixed[1, window] * filters[1, lag]
            return total
        return lax.fori_loop(0, (first + depth) // unroll, add, zeros)

    for copy in sent:
        copy.wait_recv()
    grad = arrived[:, 0]
    grads[0, :blocks] = grad
    grads[1, :blocks] = swap(grad)
    mix = arrived[:, 1]
    mixed[0, depth:] = mix
    mixed[1, depth:] = swap(mix)
    real, imag = factors(shifted(mix))
    factor[0] = real
    factor[1] = imag
    for row in range(height):
        results[0, pl.ds(row * depth, depth)] = correlate(factor, row * depth)
    sent_terms = exchange(results.at[0], returned.at[0], 1)

    for copy in passed:
        copy.wait_recv()
    whole = jnp.concatenate([filter_arrived[:, row] for row in range(height)], axis=0)
    real, imag = factors(shifted(whole))
    filters[0] = real
    filters[1] = imag
    for row in range(height):
        results[1, pl.ds(row * depth, depth)] = convolve(row * depth)
    sent_convolved = exchange(results.at[1], returned.at[1], 2)
    for row in range(height):
        results[2, pl.ds(row * depth, depth)] = correlate(filters, row * depth)
    sent_back = exchange(results.at[2], returned.at[2], 3)

    loads[9].wait()
    for copy in sent_terms:
        copy.wait_recv()
    term = inverse(returned[0].reshape(-1, LANES)) * scale
    shares[0] = term.reshape((members,) + shares.shape[2:])
    scattered = []
    for step in range(1, members):
        peer = lax.rem(member + step, members)
        scattered.append(
            send(
                shares.at[0, peer], shares.at[1, step],
                share_send.at[step], share_recv.at[step], ch=peer,
            )
        )
    for copy in scattered:
        copy.start()

    for copy in sent_convolved:
        copy.wait_recv()
    convolved_ref[...] = inverse(returned[1].reshape(-1, LANES))
    for copy in sent_back:
        copy.wait_recv()
    mixed_grad_ref[...] = inverse(returned[2].reshape(-1, LANES))

    total = shares[0, member]
    for copy in scattered:
        copy.wait_recv()
    for step in range(1, members):
        total = total + shares[1, step]
    filter_grad_ref[...] = total

    @pl.when(member != 0)
    def _():
        direct[0].wait_send()

    for copy in direct[1:] + sent + passed + sent_back + sent_terms:
        copy.wait_send()
    for copy in sent_convolved + scattered:
        copy.wait_send()


def body(queries, keys, values, filters, cotangent):
    blocks = lax.axis_size("ctx")
    members = lax.axis_size("ch")
    height = blocks // members
    rows = blocks * OWN
    share = rows // members
    tokens = queries.shape[-1]
    scale = (members * queries.shape[0] * blocks * tokens) ** -0.5
    view = lambda array: array.reshape(rows, LANES)
    arrays = [*map(view, (queries, keys, values, filters, cotangent)), *map(jnp.asarray, tables(blocks))]
    anywhere = pl.BlockSpec(memory_space=pl.ANY)
    vmem = lambda *shape: pltpu.VMEM(shape + (8, LANES), jnp.float32)
    dma = lambda *shape: pltpu.SemaphoreType.DMA(shape)
    convolved, mixed_grad, filter_grad = pl.pallas_call(
        functools.partial(kernel, blocks, members, scale),
        out_shape=[pltpu.VMEM((rows, LANES), jnp.float32)] * 2
        + [pltpu.VMEM((share, LANES), jnp.float32)],
        in_specs=[anywhere] * 10,
        out_specs=[pl.BlockSpec(memory_space=pltpu.VMEM)] * 3,
        scratch_shapes=[pltpu.VMEM(array.shape, array.dtype) for array in arrays]
        + [
            vmem(blocks, 2), vmem(blocks, 2), vmem(blocks), vmem(members, height),
            vmem(3, blocks), vmem(3, blocks),
            pltpu.VMEM((2, members, share, LANES), jnp.float32),
            vmem(2, blocks + members), vmem(2, blocks), vmem(2, blocks + members), vmem(2, blocks),
            dma(10), dma(height), dma(height), dma(members), dma(members),
            dma(4, blocks), dma(4, blocks), dma(members), dma(members),
        ],
        compiler_params=pltpu.CompilerParams(collective_id=0, has_side_effects=True),
    )(*arrays)
    convolved = convolved.reshape(queries.shape)
    mixed_grad = mixed_grad.reshape(queries.shape)
    return (
        queries * convolved, cotangent * convolved, mixed_grad * values, mixed_grad * keys,
        filter_grad.reshape(1, tokens // members),
    )


def solution(mesh):
    placed = (
        P("ch", None, "ctx"),
        P("ch", None, "ctx"),
        P("ch", None, "ctx"),
        P(None, "ctx"),
        P("ch", None, "ctx"),
    )
    return jax.shard_map(
        body,
        mesh=mesh,
        in_specs=placed,
        out_specs=(
            P("ch", None, "ctx"),
            P("ch", None, "ctx"),
            P("ch", None, "ctx"),
            P("ch", None, "ctx"),
            P(None, ("ctx", "ch")),
        ),
        check_vma=False,
    )
```
